32 devices in a mesh: layer: 4 (over y, core), row: 8 (over z, x).
Axes of the slice: x: 2, y: 2, z: 4, core: 2. Of those that a mesh axis runs over, the one named last changes fastest.
Arguments:
- rhs_leaf: float32 [8192, 128], P(('layer', 'row')), may hold values from -6 to 6
- rhs_anc: float32 [1024, 128], P('row'), may hold values from -6 to 6
- leaf_inv: float32 [64, 128, 128], P(('layer', 'row')), may hold values from -0.4 to 1.4, as said below
- leaf_low: float32 [32, 128, 128], P(('layer', 'row')), may hold values from -0.5 to 0.5
- couple: float32 [4096, 128, 128], P(('layer', 'row')), may hold values from -0.0234375 to 0.0234375
- tile_cols: int32 [32, 128], P(('layer', 'row')), may hold values from 0 to 15
- anc_inv: float32 [8, 128, 128], P('row'), may hold values from -0.4 to 1.4, as said below
- anc_low: float32 [8, 128, 128], P('row'), may hold values from -0.4375 to 0.4375
Outputs:
- leaf_solution: float32 [8192, 128], P(('layer', 'row'))
- anc_solution: float32 [1024, 128], P('row')
The draws below stay inside these ranges and needn't reach their ends.
Inputs may be any that keep to these rules, and one draw needn't show every extreme that they name: `leaf_inv`: entries of an inverse tile: the identity plus noise of at most 0.4 in size on every entry. `anc_inv`: entries of an inverse tile: the identity plus noise of at most 0.4 in size on every entry. `tile_cols`: A tile index into the leaf rows of the block's own layer; repeats allowed.
All inputs are finite; a program needn't handle non-finite values.
Results may differ from the reference program's by a relative error of at most 0.0002.
Values sent between devices are 32-bit elements; how exact they have to be, the bound alone decides.
No kernel may reach another device: no remote copies, remote signals or barrier semaphores. Data moves between devices by JAX's collectives and lax.ppermute only.
A program may use at most 64 MiB of HBM per device.

```python
import jax
import jax.numpy as jnp
from jax import lax

TILE = 128
COLS = 128
LT = 2
K = 128
BLOCKS = 32
ANC = 1024
LEAF_ALL = 8192
N_LAYER = 4
N_ROW = 8


def inverse_tiles(key, number):
    noise = jax.random.normal(key, (number, TILE, TILE), jnp.float32) * (0.5 / TILE ** 0.5)
    return jnp.clip(noise, -0.4, 0.4) + jnp.eye(TILE, dtype=jnp.float32)[None]


def draw_leaf_inv(key, part):
    return inverse_tiles(jax.random.fold_in(key, 11), BLOCKS * LT)


def draw_anc_inv(key, part):
    return inverse_tiles(jax.random.fold_in(key, 23), N_ROW)


def with_ends(entries, own_key, low, high):
    extent = entries.shape
    spot = [jax.random.randint(jax.random.fold_in(own_key, axis), (), 0, extent[axis]) for axis in range(len(extent))]
    entries = entries.at[tuple(spot)].set(low)
    longest = extent.index(max(extent))
    spot[longest] = (spot[longest] + 1) % extent[longest]
    return entries.at[tuple(spot)].set(high)


def steps_of(key, dims, split, smallest, top_value):
    factor_of, own = 1.0, jax.random.fold_in(key, 6)
    for dim, blocks in split:
        steps = jnp.exp(jax.random.uniform(jax.random.fold_in(own, dim), (blocks,), jnp.float32, smallest / len(split), top_value / len(split)))
        factor_of = factor_of * jnp.repeat(steps, dims[dim] // blocks).reshape([-1 if axis == dim else 1 for axis in range(len(dims))])
    return factor_of


def scatter_about(key, shape, spread, reach, shards=(), kind=jnp.bfloat16):
    entries = spread * jax.random.normal(key, shape, jnp.float32)
    if shards:
        entries = entries * steps_of(key, shape, shards, -0.22, 0.18)
    return jnp.clip(entries, -reach, reach).astype(kind)


def setup_inputs(seed: int = 0) -> dict:
    splits = jax.random.split(jax.random.key(seed), 9)
    return {
        "rhs_leaf": scatter_about(splits[0], (LEAF_ALL, COLS), 1.0, 6.0, ((0, 32),), jnp.float32),
        "rhs_anc": scatter_about(splits[1], (ANC, COLS), 1.0, 6.0, ((0, 8),), jnp.float32),
        "leaf_inv": draw_leaf_inv(jax.random.fold_in(splits[8], 71), 0),
        "leaf_low": scatter_about(splits[3], (BLOCKS * (LT - 1), TILE, TILE), TILE ** -0.5, 0.5, ((0, 32),), jnp.float32),
        "couple": scatter_about(splits[4], (BLOCKS * K, TILE, TILE), (TILE * K * N_LAYER) ** -0.5, 0.0234375, ((0, 32),), jnp.float32),
        "tile_cols": with_ends(jax.random.randint(splits[5], (BLOCKS, K), 0, N_ROW * LT), jax.random.fold_in(splits[5], 1), 0, (N_ROW * LT) - 1).astype(jnp.int32),
        "anc_inv": draw_anc_inv(jax.random.fold_in(splits[8], 71), 0),
        "anc_low": scatter_about(splits[7], (N_ROW, TILE, TILE), (TILE * 7 // 5) ** -0.5, 0.4375, ((0, 8),), jnp.float32),
    }


highest = lax.Precision.HIGHEST


def reference(rhs_leaf, rhs_anc, leaf_inv, leaf_low, couple, tile_cols, anc_inv, anc_low):
    layer_tiles = N_ROW * LT
    right_side = rhs_leaf.reshape(BLOCKS, LT, TILE, COLS)
    inverse = leaf_inv.reshape(BLOCKS, LT, TILE, TILE)
    lower = leaf_low.reshape(BLOCKS, LT - 1, TILE, TILE)
    forward = []
    for tile_pos in range(LT):
        source = right_side[:, tile_pos]
        if tile_pos > 0:
            source = source - jnp.einsum('bij,bjc->bic', lower[:, tile_pos - 1], forward[-1], precision=highest)
        forward.append(jnp.einsum('bij,bjc->bic', inverse[:, tile_pos], source, precision=highest))
    solved = jnp.stack(forward, axis=1)
    layer_view = solved.reshape(N_LAYER, layer_tiles, TILE, COLS)
    coupling = couple.reshape(BLOCKS, K, TILE, TILE)
    layer_ids = (jnp.arange(BLOCKS) // N_ROW).astype(jnp.int32)
    row_ids = (jnp.arange(BLOCKS) % N_ROW).astype(jnp.int32)

    def partial_sum(block_items):
        tile_stack, columns, layer_id = block_items
        picked = layer_view[layer_id][columns]
        return jnp.einsum('kab,kbc->ac', tile_stack, picked, precision=highest)

    partials = lax.map(partial_sum, (coupling, tile_cols, layer_ids))
    summed = partials.reshape(N_LAYER, N_ROW, TILE, COLS).sum(axis=0)
    anc_right = rhs_anc.reshape(N_ROW, TILE, COLS)

    def ahead_step(previous, block_items):
        inv_tile, low_tile, right_tile, summed_tile = block_items
        inner = right_tile - summed_tile - jnp.dot(low_tile, previous, precision=highest)
        current = jnp.dot(inv_tile, inner, precision=highest)
        return current, current

    zero_tile = jnp.zeros((TILE, COLS), jnp.float32)
    unused_one, ahead_out = lax.scan(ahead_step, zero_tile, (anc_inv, anc_low, anc_right, summed))
    low_next = jnp.concatenate([anc_low[1:], jnp.zeros((1, TILE, TILE), jnp.float32)], axis=0)

    def behind_step(following, block_items):
        inv_tile, low_tile, ahead_tile = block_items
        inner = ahead_tile - jnp.dot(low_tile.T, following, precision=highest)
        current = jnp.dot(inv_tile.T, inner, precision=highest)
        return current, current

    unused_two, behind_out = lax.scan(behind_step, zero_tile, (anc_inv, low_next, ahead_out), reverse=True)

    def scatter_back(accumulated, block_items):
        tile_stack, columns, layer_id, row_id = block_items
        contrib = jnp.einsum('kba,bc->kac', tile_stack, behind_out[row_id], precision=highest)
        return accumulated.at[layer_id, columns].add(contrib), None

    start_acc = jnp.zeros((N_LAYER, layer_tiles, TILE, COLS), jnp.float32)
    updates, unused_three = lax.scan(scatter_back, start_acc, (coupling, tile_cols, layer_ids, row_ids))
    target = solved - updates.reshape(BLOCKS, LT, TILE, COLS)
    backward = [None] * LT
    for tile_pos in range(LT - 1, -1, -1):
        source = target[:, tile_pos]
        if tile_pos < LT - 1:
            source = source - jnp.einsum('bji,bjc->bic', lower[:, tile_pos], backward[tile_pos + 1], precision=highest)
        backward[tile_pos] = jnp.einsum('bji,bjc->bic', inverse[:, tile_pos], source, precision=highest)
    leaf_solution = jnp.stack(backward, axis=1).reshape(BLOCKS * LT * TILE, COLS)
    return leaf_solution, behind_out.reshape(N_ROW * TILE, COLS)
```

```python
import functools

import jax
import jax.numpy as jnp
from jax import lax
from jax.experimental import pallas as pl
from jax.experimental.pallas import tpu as pltpu
from jax.sharding import PartitionSpec as P


F32 = jnp.float32
VM = pl.BlockSpec(memory_space=pltpu.VMEM)
SM = pl.BlockSpec(memory_space=pltpu.SMEM)


def dot(a, b):
    return jnp.dot(a, b, precision=lax.Precision.HIGHEST, preferred_element_type=F32)


def shape(*dims):
    return jax.ShapeDtypeStruct(dims, F32)


def call(body, name, outs, ins, scratch=()):
    return pl.pallas_call(
        body, name=name, out_shape=outs, in_specs=[VM] * len(ins),
        out_specs=jax.tree.map(lambda _: VM, outs), scratch_shapes=list(scratch),
    )(*ins)


def pair_swap(value, axis, distance):
    count = lax.axis_size(axis)
    return lax.ppermute(value, axis, [(i, i ^ distance) for i in range(count)])


def leaf_forward(rhs, inv, low, a_tile, l_tile, msg):
    tile = inv.shape[1]
    half = tile // 2
    core = lax.axis_index("layer") % 2
    above = None
    for t in range(inv.shape[0]):
        source = rhs[t * tile:(t + 1) * tile, :]
        if t > 0:
            source = source - dot(low[t - 1], above)
        above = dot(inv[t], source)
        msg[t * tile:(t + 1) * tile, :] = above
    base = inv.shape[0] * tile
    start = pl.multiple_of(core * half, half)
    msg[base:base + half, :] = a_tile[0, pl.ds(start, half), :]
    msg[base + half:base + tile, :] = l_tile[0, pl.ds(start, half), :]


def merge_body(leaf_tiles, cols, couple, same, *rest):
    step = pl.program_id(0)
    place = lax.axis_index("row")
    per_step = couple.shape[0]
    acc = rest[-1]
    outs = rest[:-1]

    @pl.when(step == 0)
    def _():
        acc[...] = jnp.zeros_like(acc)

    def one(i, carry):
        col = cols[0, step * per_step + i]
        owner = lax.div(col, leaf_tiles)
        acc[(owner ^ place) * leaf_tiles + col - owner * leaf_tiles] += couple[i]
        return carry

    lax.fori_loop(0, per_step, one, 0, unroll=4)

    @pl.when(step == pl.num_programs(0) - 1)
    def _():
        far = acc.shape[0] // (2 * leaf_tiles)
        for t in range(leaf_tiles):
            same[t] = acc[t]
            for k in range(far):
                base = 2 * k * leaf_tiles + t
                if k > 0:
                    outs[k - 1][t] = acc[base]
                outs[-1][k, t] = acc[base + leaf_tiles]


def merge(couple, cols, leaf_tiles):
    k_all, tile, _ = couple.shape
    rows = lax.axis_size("row")
    far = rows // 2
    per_step = min(k_all, 16)
    piece = shape(leaf_tiles, tile, tile)
    outs = [piece] * far + [shape(far, leaf_tiles, tile, tile)]
    return pl.pallas_call(
        functools.partial(merge_body, leaf_tiles), name="merge_couple",
        grid=(k_all // per_step,),
        in_specs=[SM, pl.BlockSpec((per_step, tile, tile), lambda i: (i, 0, 0))],
        out_specs=[VM] * len(outs), out_shape=outs,
        scratch_shapes=[pltpu.VMEM((rows * leaf_tiles, tile, tile), F32)],
    )(cols, couple)


def partial_body(count, leaf_tiles, *refs):
    msgs, mats = refs[:count], refs[count:2 * count]
    anc, own, other, right = refs[2 * count:2 * count + 4]
    buf = refs[-1]
    tile = mats[0].shape[1]
    half = tile // 2
    core = lax.axis_index("layer") % 2
    total = None
    for msg, mat in zip(msgs, mats):
        for t in range(leaf_tiles):
            term = dot(mat[t], msg[t * tile:(t + 1) * tile, :])
            total = term if total is None else total + term
    mine = pl.multiple_of(core * half, half)
    theirs = pl.multiple_of((1 - core) * half, half)
    buf[...] = total.T
    own[...] = buf[pl.ds(mine, half), :]
    other[...] = buf[pl.ds(theirs, half), :]
    buf[...] = anc[...].T
    right[...] = buf[pl.ds(mine, half), :]


def factor_body(count, far, mine, theirs, *refs):
    at_out, a_out, tt_out, s_out, l_buf = refs
    tile = a_out.shape[1]
    half = tile // 2
    core = lax.axis_index("layer") % 2
    place = lax.axis_index("row")
    up = pl.multiple_of(core * half, half)
    down = pl.multiple_of((1 - core) * half, half)
    for i in range(count):
        r = place ^ i
        a_out[r, pl.ds(up, half), :] = mine[i, :half, :]
        a_out[r, pl.ds(down, half), :] = theirs[i, :half, :]
        l_buf[r, pl.ds(up, half), :] = mine[i, half:, :]
        l_buf[r, pl.ds(down, half), :] = theirs[i, half:, :]

    def one(r, carry):
        a = a_out[r]
        at_out[r] = a.T
        tt_out[r] = dot(a, l_buf[r]).T
        s_out[r] = dot(l_buf[jnp.minimum(r + 1, count - 1)], a)
        return carry

    lax.fori_loop(0, count, one, 0)


def solve_body(count, *refs):
    pieces = refs[:count]
    at, a, tt, s, z, buf = refs[count:]
    place = lax.axis_index("row")
    for i in range(count):
        buf[place ^ i] = pieces[i][...]
    c = [dot(buf[r], at[r]) for r in range(count)]
    y = [c[0]]
    for r in range(1, count):
        y.append(c[r] - dot(y[-1], tt[r]))
    d = [dot(y[r], a[r]) for r in range(count)]
    behind = d[-1]
    z[count - 1] = behind
    for r in range(count - 2, -1, -1):
        behind = d[r] - dot(behind, s[r])
        z[r] = behind


def final_body(count, leaf_tiles, *refs):
    z_mine, z_theirs, x, inv, low = refs[:5]
    mats = refs[5:5 + count]
    leaf, anc, zt = refs[5 + count:]
    tile = inv.shape[1]
    half = tile // 2
    core = lax.axis_index("layer") % 2
    place = lax.axis_index("row")
    zt[:, pl.ds(pl.multiple_of(core * half, half), half), :] = z_mine[...]
    zt[:, pl.ds(pl.multiple_of((1 - core) * half, half), half), :] = z_theirs[...]
    anc[...] = zt[place].T
    q = [x[t * tile:(t + 1) * tile, :].T for t in range(leaf_tiles)]
    for i in range(count):
        left = zt[place ^ i]
        for t in range(leaf_tiles):
            q[t] = q[t] - dot(left, mats[i][t])
    below = None
    for t in range(leaf_tiles - 1, -1, -1):
        source = q[t]
        if below is not None:
            source = source - dot(below, low[t])
        below = dot(source, inv[t])
        leaf[t * tile:(t + 1) * tile, :] = below.T


def gather_row(msg, far):
    near = pair_swap(msg, "row", 1)
    straight = [pair_swap(msg, "row", 2 * k) for k in range(far - 1, 0, -1)][::-1]
    crossed = [pair_swap(piece, "row", 1) for piece in straight]
    out = [msg, near]
    for k in range(1, far):
        out += [straight[k - 1], crossed[k - 1]]
    return out


def per_device(rhs_leaf, rhs_anc, leaf_inv, leaf_low, couple, tile_cols, anc_inv, anc_low):
    leaf_tiles, tile, _ = leaf_inv.shape
    cols = rhs_leaf.shape[1]
    half = cols // 2
    count = lax.axis_size("row")
    far = count // 2
    decks = lax.axis_size("layer") // 2
    base = leaf_tiles * tile

    ins = (rhs_leaf, leaf_inv, leaf_low, anc_inv, anc_low)
    msg = call(leaf_forward, "leaf_forward", shape(base + tile, cols), ins)
    msgs = gather_row(msg, far)

    *straight, crossed = merge(couple, tile_cols, leaf_tiles)
    mats = []
    for k in range(far):
        mats += [straight[k], crossed[k]]

    came = pair_swap(crossed, "row", 1)
    columns = [straight[0], came[0]]
    for k in range(1, far):
        got = pair_swap(jnp.stack([straight[k], came[k]]), "row", 2 * k)
        columns += [got[0], got[1]]

    ins = (*msgs, *mats, rhs_anc)
    own, other, right = call(
        functools.partial(partial_body, count, leaf_tiles), "partial_sum",
        [shape(half, tile)] * 3, ins, [pltpu.VMEM((cols, tile), F32)],
    )
    part = own + pair_swap(other, "layer", 1)
    total = part
    for k in range(1, decks):
        total = total + pair_swap(part, "layer", 2 * k)
    pieces = gather_row(right - total, far)

    mine = jnp.stack([m[base:] for m in msgs])
    theirs = pair_swap(mine, "layer", 1)
    at, a, tt, s = call(
        functools.partial(factor_body, count, far), "factors",
        [shape(count, tile, tile)] * 4, (mine, theirs), [pltpu.VMEM((count, tile, tile), F32)],
    )
    z_mine = call(
        functools.partial(solve_body, count), "ancestor_solve", shape(count, half, tile),
        (*pieces, at, a, tt, s), [pltpu.VMEM((count, half, tile), F32)],
    )
    z_theirs = pair_swap(z_mine, "layer", 1)
    return call(
        functools.partial(final_body, count, leaf_tiles), "leaf_backward",
        (shape(base, cols), shape(tile, cols)),
        (z_mine, z_theirs, msg, leaf_inv, leaf_low, *columns),
        [pltpu.VMEM((count, cols, tile), F32)],
    )


def solution(mesh):
    placed = (
        P(("layer", "row"), None),
        P("row", None),
        P(("layer", "row"), None, None),
        P(("layer", "row"), None, None),
        P(("layer", "row"), None, None),
        P(("layer", "row"), None),
        P("row", None, None),
        P("row", None, None),
    )
    return jax.shard_map(
        per_device,
        mesh=mesh,
        in_specs=placed,
        out_specs=(P(("layer", "row"), None), P("row", None)),
        check_vma=False,
    )
```

```python
import functools
import math

import jax
import jax.numpy as jnp
from jax import lax
from jax.experimental import pallas as pl
from jax.experimental.pallas import tpu as pltpu
from jax.sharding import PartitionSpec as P


F32 = jnp.float32
VM = pl.BlockSpec(memory_space=pltpu.VMEM)
SM = pl.BlockSpec(memory_space=pltpu.SMEM)


def split(value, axis):
    high = value.astype(jnp.bfloat16)
    low = (value - high.astype(F32)).astype(jnp.bfloat16)
    return jnp.concatenate([high, low], axis=axis)


def spread(left, wide):
    rows, width = left.shape[0], wide.shape[1] // 2
    out = jnp.dot(split(left, 0), wide, preferred_element_type=F32)
    cross = out[:rows, width:] + out[rows:, :width]
    return out[:rows, :width] + (cross + out[rows:, width:])


def dot(left, right):
    return spread(left, split(right, 1))


def shape(*dims, dtype=F32):
    return jax.ShapeDtypeStruct(dims, dtype)


def room(scratch, outs=()):
    arrays = [v for v in [*scratch, *outs] if v.dtype in (F32, jnp.bfloat16)]
    size = sum(math.prod(v.shape) * jnp.dtype(v.dtype).itemsize for v in arrays)
    return pltpu.CompilerParams(vmem_limit_bytes=2 * size + (6 << 20))


def call(body, outs, far=(), arrived=(), scratch=(), stay=False):
    arrived = [pltpu.with_memory_space_constraint(v, pltpu.VMEM) for v in arrived]
    if stay:
        outs = [pltpu.VMEM(o.shape, o.dtype) for o in outs]
    copies = [pltpu.VMEM(v.shape, v.dtype) for v in far]
    if far:
        copies.append(pltpu.SemaphoreType.DMA((len(far),)))
    scratch = copies + list(scratch)
    return pl.pallas_call(
        body, out_shape=list(outs), compiler_params=room(scratch, outs),
        in_specs=[pl.BlockSpec(memory_space=pl.ANY)] * len(far) + [VM] * len(arrived),
        out_specs=[VM] * len(outs), scratch_shapes=scratch,
    )(*far, *arrived)


def fetch(sources, copies):
    started = [
        pltpu.make_async_copy(source, target, copies[len(sources)].at[i])
        for i, (source, target) in enumerate(zip(sources, copies))
    ]
    for copy in started:
        copy.start()

    def ready(i):
        started[i].wait()
        return copies[i]

    return ready


def pair_swap(value, axis, distance):
    count = lax.axis_size(axis)
    return lax.ppermute(value, axis, [(i, i ^ distance) for i in range(count)])


def leaf_body(*refs):
    ready = fetch(refs[:5], refs[7:])
    msg, anc = refs[5:7]
    tile = msg.shape[1]
    tiles = msg.shape[0] // tile
    half = tile // 2
    core = lax.axis_index("layer") % 2
    rhs, inv, low = ready(0), ready(1), ready(2)
    above = None
    for t in range(tiles):
        source = rhs[t * tile:(t + 1) * tile, :]
        if t > 0:
            source = source - dot(low[t - 1], above)
        above = dot(inv[t], source)
        msg[t * tile:(t + 1) * tile, :] = above
    start = pl.multiple_of(core * half, half)
    anc[:half, :] = ready(3)[0, pl.ds(start, half), :]
    anc[half:, :] = ready(4)[0, pl.ds(start, half), :]


def merge_body(leaf_tiles, chunk, cols, couple, *rest):
    place = lax.axis_index("row")
    outs, (buf, acc_a, acc_b, sems) = rest[:-4], rest[-4:]
    parts = couple.shape[0] // chunk
    started = [
        pltpu.make_async_copy(
            couple.at[pl.ds(i * chunk, chunk)], buf.at[pl.ds(i * chunk, chunk)], sems.at[i])
        for i in range(parts)
    ]
    for copy in started:
        copy.start()
    acc_a[...] = jnp.zeros_like(acc_a)
    acc_b[...] = jnp.zeros_like(acc_b)

    def add(acc, k):
        col = cols[0, k]
        owner = lax.div(col, leaf_tiles)
        acc[(owner ^ place) * leaf_tiles + col - owner * leaf_tiles] += buf[k]

    for i in range(parts):
        started[i].wait()

        def one(j, carry):
            add(acc_a, i * chunk + 2 * j)
            add(acc_b, i * chunk + 2 * j + 1)
            return carry

        lax.fori_loop(0, chunk // 2, one, 0, unroll=4)
    for i, out in enumerate(outs):
        for t in range(leaf_tiles):
            out[t] = acc_a[i * leaf_tiles + t] + acc_b[i * leaf_tiles + t]


def merge(couple, cols, leaf_tiles):
    k_all, tile, _ = couple.shape
    rows = lax.axis_size("row")
    chunk = 16 if k_all % 16 == 0 else k_all
    acc = pltpu.VMEM((rows * leaf_tiles, tile, tile), F32)
    scratch = [pltpu.VMEM(couple.shape, F32), acc, acc]
    return pl.pallas_call(
        functools.partial(merge_body, leaf_tiles, chunk), name="merge",
        in_specs=[SM, pl.BlockSpec(memory_space=pl.ANY)],
        out_specs=[VM] * rows, out_shape=[pltpu.VMEM((leaf_tiles, tile, tile), F32)] * rows,
        compiler_params=room(scratch),
        scratch_shapes=scratch + [pltpu.SemaphoreType.DMA((k_all // chunk,))],
    )(cols, couple)


def partial_body(count, *refs):
    ready = fetch(refs[:2], refs[2 * count + 4:])
    mats, msgs = refs[2:2 + count], refs[2 + count:1 + 2 * count]
    own, other, right = refs[1 + 2 * count:4 + 2 * count]
    buf = refs[-1]
    leaf_tiles, tile, _ = mats[0].shape
    half = tile // 2
    core = lax.axis_index("layer") % 2
    wide, thin = None, None
    for i in list(range(1, count)) + [0]:
        msg = msgs[i - 1] if i else ready(0)
        right_side = split(msg[...], 1)
        row = jnp.concatenate([mats[i][t] for t in range(leaf_tiles)], axis=1)
        high = row.astype(jnp.bfloat16)
        low = (row - high.astype(F32)).astype(jnp.bfloat16)
        a = jnp.dot(high, right_side, preferred_element_type=F32)
        b = jnp.dot(low, right_side[:, :right_side.shape[1] // 2], preferred_element_type=F32)
        wide = a if wide is None else wide + a
        thin = b if thin is None else thin + b
    cols = thin.shape[1]
    total = wide[:, :cols] + (wide[:, cols:] + thin)
    up = pl.multiple_of(core * half, half)
    down = pl.multiple_of((1 - core) * half, half)
    buf[...] = total.T
    own[...] = buf[pl.ds(up, half), :]
    other[...] = buf[pl.ds(down, half), :]
    buf[...] = ready(1)[...].T
    right[...] = buf[pl.ds(up, half), :]


def stack_body(*refs):
    ready = fetch(refs[:1], refs[-2:])
    out = refs[-3]
    for i in range(1, len(refs) - 3):
        out[i] = refs[i][...]
    out[0] = ready(0)[...]


def solve_body(count, *refs):
    mine, theirs = refs[:2]
    pieces = refs[2:2 + count]
    z, buf, a_buf, l_buf = refs[2 + count:]
    tile = a_buf.shape[1]
    half = tile // 2
    core = lax.axis_index("layer") % 2
    place = lax.axis_index("row")
    up = pl.multiple_of(core * half, half)
    down = pl.multiple_of((1 - core) * half, half)
    for i in range(count):
        r = place ^ i
        a_buf[r, pl.ds(up, half), :] = mine[i, :half, :]
        a_buf[r, pl.ds(down, half), :] = theirs[i, :half, :]
        l_buf[r, pl.ds(up, half), :] = mine[i, half:, :]
        l_buf[r, pl.ds(down, half), :] = theirs[i, half:, :]
        buf[r] = pieces[i][...]
    a = [split(a_buf[r], 1) for r in range(count)]
    y = []
    for r in range(count):
        value = spread(buf[r], split(a_buf[r].T, 1))
        if r > 0:
            value = value - dot(y[-1], spread(a_buf[r], split(l_buf[r], 1)).T)
        y.append(value)
    behind = None
    for r in range(count - 1, -1, -1):
        value = spread(y[r], a[r])
        if behind is not None:
            value = value - dot(behind, spread(l_buf[r + 1], a[r]))
        behind = value
        z[r] = behind


def final_body(count, *refs):
    ready = fetch(refs[:4], refs[7 + count:])
    z_mine, z_theirs = refs[4:6]
    mats = refs[6:5 + count]
    leaf, anc = refs[5 + count:7 + count]
    zt = refs[-1]
    leaf_tiles, tile, _ = refs[0].shape
    half = tile // 2
    core = lax.axis_index("layer") % 2
    place = lax.axis_index("row")
    zt[:, pl.ds(pl.multiple_of(core * half, half), half), :] = z_mine[...]
    zt[:, pl.ds(pl.multiple_of((1 - core) * half, half), half), :] = z_theirs[...]
    anc[...] = zt[place].T
    cols = zt.shape[1]
    both, single = None, None
    for i in list(range(1, count)) + [0]:
        mat = mats[i - 1] if i else ready(0)
        left = split(zt[place ^ i], 0)
        row = jnp.concatenate([mat[t] for t in range(leaf_tiles)], axis=1)
        high = row.astype(jnp.bfloat16)
        low_part = (row - high.astype(F32)).astype(jnp.bfloat16)
        p = jnp.dot(left, high, preferred_element_type=F32)
        q = jnp.dot(left[:cols], low_part, preferred_element_type=F32)
        both = p if both is None else both + p
        single = q if single is None else single + q
    total = both[:cols] + (both[cols:] + single)
    x, inv, low = ready(1), ready(2), ready(3)
    below = None
    for t in range(leaf_tiles - 1, -1, -1):
        rows = slice(t * tile, (t + 1) * tile)
        source = x[rows, :].T - total[:, rows]
        if below is not None:
            source = source - dot(below, low[t])
        below = dot(source, inv[t])
        leaf[rows, :] = below.T


def gather_row(msg, far):
    out = [msg, None] + [None] * (2 * far - 2)
    for k in range(far - 1, 0, -1):
        out[2 * k] = pair_swap(msg, "row", 2 * k)
    for k in range(far):
        out[2 * k + 1] = pair_swap(out[2 * k], "row", 1)
    return out


def per_device(rhs_leaf, rhs_anc, leaf_inv, leaf_low, couple, tile_cols, anc_inv, anc_low):
    leaf_tiles, tile, _ = leaf_inv.shape
    cols = rhs_leaf.shape[1]
    half = cols // 2
    count = lax.axis_size("row")
    far = count // 2
    decks = lax.axis_size("layer") // 2
    base = leaf_tiles * tile

    msg, anc = call(
        leaf_body, (shape(base, cols), shape(tile, tile)),
        (rhs_leaf, leaf_inv, leaf_low, anc_inv, anc_low), stay=True,
    )
    msgs = gather_row(msg, far)
    ancs = gather_row(anc, far)
    mats = merge(couple, tile_cols, leaf_tiles)
    columns = [pair_swap(mats[i], "row", i) for i in range(1, count)]

    own, other, right = call(
        functools.partial(partial_body, count), [shape(half, tile)] * 3,
        (msg, rhs_anc), (*mats, *msgs[1:]), [pltpu.VMEM((cols, tile), F32)], stay=True,
    )
    part = own + pair_swap(other, "layer", 1)
    total = part
    for k in range(1, decks):
        total = total + pair_swap(part, "layer", 2 * k)
    pieces = gather_row(right - total, far)

    mine, = call(stack_body, [shape(count, tile, tile)], (anc,), ancs[1:], stay=True)
    theirs = pair_swap(mine, "layer", 1)
    z_mine, = call(
        functools.partial(solve_body, count), [shape(count, half, tile)],
        (), (mine, theirs, *pieces),
        [pltpu.VMEM((count, half, tile), F32)] + [pltpu.VMEM((count, tile, tile), F32)] * 2,
        stay=True,
    )
    z_theirs = pair_swap(z_mine, "layer", 1)
    leaf, anc_out = call(
        functools.partial(final_body, count),
        (shape(base, cols), shape(tile, cols)),
        (mats[0], msg, leaf_inv, leaf_low), (z_mine, z_theirs, *columns),
        [pltpu.VMEM((count, cols, tile), F32)],
    )
    return leaf, anc_out


def solution(mesh):
    placed = (
        P(("layer", "row"), None),
        P("row", None),
        P(("layer", "row"), None, None),
        P(("layer", "row"), None, None),
        P(("layer", "row"), None, None),
        P(("layer", "row"), None),
        P("row", None, None),
        P("row", None, None),
    )

    return jax.shard_map(
        per_device,
        mesh=mesh,
        in_specs=placed,
        out_specs=(P(("layer", "row"), None), P("row", None)),
        check_vma=False,
    )
```

```python
import functools
import math

import jax
import jax.numpy as jnp
from jax import lax
from jax.experimental import pallas as pl
from jax.experimental.pallas import tpu as pltpu
from jax.sharding import PartitionSpec as P


F32 = jnp.float32
VM = pl.BlockSpec(memory_space=pltpu.VMEM)
HB = pl.BlockSpec(memory_space=pltpu.HBM)
SM = pl.BlockSpec(memory_space=pltpu.SMEM)


def split(value, axis):
    high = value.astype(jnp.bfloat16)
    low = (value - high.astype(F32)).astype(jnp.bfloat16)
    return jnp.concatenate([high, low], axis=axis)


def spread(left, wide):
    rows, width = left.shape[0], wide.shape[1] // 2
    out = jnp.dot(split(left, 0), wide, preferred_element_type=F32)
    cross = out[:rows, width:] + out[rows:, :width]
    return out[:rows, :width] + (cross + out[rows:, width:])


def dot(left, right):
    return spread(left, split(right, 1))


def shape(*dims, dtype=F32):
    return jax.ShapeDtypeStruct(dims, dtype)


def room(scratch, outs=()):
    arrays = [v for v in [*scratch, *outs] if v.dtype in (F32, jnp.bfloat16)]
    size = sum(math.prod(v.shape) * jnp.dtype(v.dtype).itemsize for v in arrays)
    return pltpu.CompilerParams(vmem_limit_bytes=2 * size + (6 << 20))


def call(body, outs, far=(), arrived=(), scratch=(), stay=False):
    far = [pltpu.with_memory_space_constraint(v, pltpu.HBM) for v in far]
    arrived = [pltpu.with_memory_space_constraint(v, pltpu.VMEM) for v in arrived]
    if stay:
        outs = [pltpu.VMEM(o.shape, o.dtype) for o in outs]
    copies = [pltpu.VMEM(v.shape, v.dtype) for v in far]
    if far:
        copies.append(pltpu.SemaphoreType.DMA((len(far),)))
    scratch = copies + list(scratch)
    return pl.pallas_call(
        body, out_shape=list(outs), compiler_params=room(scratch, outs),
        in_specs=[HB] * len(far) + [VM] * len(arrived),
        out_specs=[VM] * len(outs), scratch_shapes=scratch,
    )(*far, *arrived)


def fetch(sources, copies):
    started = [
        pltpu.make_async_copy(source, target, copies[len(sources)].at[i])
        for i, (source, target) in enumerate(zip(sources, copies))
    ]
    for copy in started:
        copy.start()

    def ready(i):
        started[i].wait()
        return copies[i]

    return ready


def pair_swap(value, axis, distance):
    count = lax.axis_size(axis)
    return lax.ppermute(value, axis, [(i, i ^ distance) for i in range(count)])


def leaf_body(*refs):
    ready = fetch(refs[:6], refs[8:])
    inv_far, (msg, right) = refs[1], refs[6:8]
    buf = refs[-1]
    tile = msg.shape[1]
    tiles = inv_far.shape[0]
    half = tile // 2
    share = tile // lax.axis_size("layer")
    base = tiles * tile
    own = pl.multiple_of(lax.axis_index("layer") * share, share)
    start = pl.multiple_of(lax.axis_index("layer") % 2 * half, half)
    rhs, inv, low = ready(0), ready(1), ready(2)
    above = None
    for t in range(tiles):
        source = rhs[t * tile:(t + 1) * tile, :]
        if t > 0:
            source = source - dot(low[t - 1], above)
        above = dot(inv[t], source)
        msg[t * tile:(t + 1) * tile, :] = above
    msg[base:base + share, :] = ready(3)[0, pl.ds(own, share), :]
    msg[base + share:, :] = ready(4)[0, pl.ds(own, share), :]
    buf[...] = ready(5)[...].T
    right[...] = buf[pl.ds(start, half), :]


def merge_body(leaf_tiles, chunk, cols_far, couple, *rest):
    place = lax.axis_index("row")
    outs, (buf, acc_a, acc_b, cols, sems) = rest[:-5], rest[-5:]
    parts = couple.shape[0] // chunk
    table = pltpu.make_async_copy(cols_far, cols, sems.at[parts])
    table.start()
    started = [
        pltpu.make_async_copy(
            couple.at[pl.ds(i * chunk, chunk)], buf.at[pl.ds(i * chunk, chunk)], sems.at[i])
        for i in range(parts)
    ]
    for copy in started:
        copy.start()
    acc_a[...] = jnp.zeros_like(acc_a)
    acc_b[...] = jnp.zeros_like(acc_b)
    table.wait()

    def add(acc, k):
        col = cols[0, k]
        owner = lax.div(col, leaf_tiles)
        acc[(owner ^ place) * leaf_tiles + col - owner * leaf_tiles] += buf[k]

    for i in range(parts):
        started[i].wait()

        def one(j, carry):
            add(acc_a, i * chunk + 2 * j)
            add(acc_b, i * chunk + 2 * j + 1)
            return carry

        lax.fori_loop(0, chunk // 2, one, 0, unroll=4)
    for i, out in enumerate(outs):
        for t in range(leaf_tiles):
            out[t] = acc_a[i * leaf_tiles + t] + acc_b[i * leaf_tiles + t]


def merge(couple, cols, leaf_tiles):
    k_all, tile, _ = couple.shape
    rows = lax.axis_size("row")
    chunk = 16 if k_all % 16 == 0 else k_all
    acc = pltpu.VMEM((rows * leaf_tiles, tile, tile), F32)
    scratch = [pltpu.VMEM(couple.shape, F32), acc, acc]
    return pl.pallas_call(
        functools.partial(merge_body, leaf_tiles, chunk), name="merge",
        in_specs=[HB, HB],
        out_specs=[VM] * rows, out_shape=[pltpu.VMEM((leaf_tiles, tile, tile), F32)] * rows,
        compiler_params=room(scratch),
        scratch_shapes=scratch + [
            pltpu.SMEM(cols.shape, jnp.int32), pltpu.SemaphoreType.DMA((k_all // chunk + 1,))],
    )(*[pltpu.with_memory_space_constraint(v, pltpu.HBM) for v in (cols, couple)])


def partial_body(count, *refs):
    mats, msgs = refs[:count], refs[count:2 * count]
    own, other, mine, buf = refs[2 * count:]
    leaf_tiles, tile, _ = mats[0].shape
    half = tile // 2
    core = lax.axis_index("layer") % 2
    wide, thin = None, None
    for i in range(count):
        mine[i] = msgs[i][leaf_tiles * tile:, :]
        right_side = split(msgs[i][:leaf_tiles * tile, :], 1)
        row = jnp.concatenate([mats[i][t] for t in range(leaf_tiles)], axis=1)
        high = row.astype(jnp.bfloat16)
        low = (row - high.astype(F32)).astype(jnp.bfloat16)
        a = jnp.dot(high, right_side, preferred_element_type=F32)
        b = jnp.dot(low, right_side[:, :right_side.shape[1] // 2], preferred_element_type=F32)
        wide = a if wide is None else wide + a
        thin = b if thin is None else thin + b
    cols = thin.shape[1]
    total = wide[:, :cols] + (wide[:, cols:] + thin)
    up = pl.multiple_of(core * half, half)
    down = pl.multiple_of((1 - core) * half, half)
    buf[...] = total.T
    own[...] = buf[pl.ds(up, half), :]
    other[...] = buf[pl.ds(down, half), :]


def stack_body(*refs):
    at = 0
    for ref in refs[:-1]:
        if len(ref.shape) == len(refs[-1].shape):
            refs[-1][at:at + ref.shape[0]] = ref[...]
            at += ref.shape[0]
        else:
            refs[-1][at] = ref[...]
            at += 1


def factor_body(*refs):
    parts = refs[:-6]
    at, a, tt, s, a_buf, l_buf = refs[-6:]
    count, tile, _ = a_buf.shape
    share = tile // len(parts)
    layer = lax.axis_index("layer")
    place = lax.axis_index("row")
    for j, part in enumerate(parts):
        rows = pl.ds(pl.multiple_of((layer ^ j) * share, share), share)
        for i in range(count):
            a_buf[place ^ i, rows, :] = part[i, :share, :]
            l_buf[place ^ i, rows, :] = part[i, share:, :]
    for r in range(count):
        wide = split(a_buf[r], 1)
        a[r] = wide
        at[r] = split(a_buf[r].T, 1)
        if r > 0:
            tt[r] = split(dot(a_buf[r], l_buf[r]).T, 1)
        if r < count - 1:
            s[r] = split(spread(l_buf[r + 1], wide), 1)


def solve_body(steps, *refs):
    at, a, tt, s = refs[:4]
    right = refs[4:6]
    z, buf = refs[6:]
    count = buf.shape[0]
    place = lax.axis_index("row")
    for near in range(2):
        for p, k in enumerate(steps):
            buf[place ^ (2 * k + near)] = right[near][p]
    c = [spread(buf[r], at[r]) for r in range(count)]
    y = [c[0]]
    for r in range(1, count):
        y.append(c[r] - spread(y[-1], tt[r]))
    d = [spread(y[r], a[r]) for r in range(count)]
    behind = d[-1]
    z[count - 1] = behind
    for r in range(count - 2, -1, -1):
        behind = d[r] - spread(behind, s[r])
        z[r] = behind


def final_body(count, *refs):
    ready = fetch(refs[:2], refs[7 + count:])
    z_mine, z_theirs, x = refs[2:5]
    mats = refs[5:5 + count]
    leaf, anc = refs[5 + count:7 + count]
    zt = refs[-1]
    leaf_tiles, tile, _ = refs[0].shape
    half = tile // 2
    core = lax.axis_index("layer") % 2
    place = lax.axis_index("row")
    zt[:, pl.ds(pl.multiple_of(core * half, half), half), :] = z_mine[...]
    zt[:, pl.ds(pl.multiple_of((1 - core) * half, half), half), :] = z_theirs[...]
    anc[...] = zt[place].T
    cols = zt.shape[1]
    both, single = None, None
    for i, mat in enumerate(mats):
        left = split(zt[place ^ i], 0)
        row = jnp.concatenate([mat[t] for t in range(leaf_tiles)], axis=1)
        high = row.astype(jnp.bfloat16)
        low_part = (row - high.astype(F32)).astype(jnp.bfloat16)
        p = jnp.dot(left, high, preferred_element_type=F32)
        q = jnp.dot(left[:cols], low_part, preferred_element_type=F32)
        both = p if both is None else both + p
        single = q if single is None else single + q
    total = both[:cols] + (both[cols:] + single)
    inv, low = ready(0), ready(1)
    below = None
    for t in range(leaf_tiles - 1, -1, -1):
        rows = slice(t * tile, (t + 1) * tile)
        source = x[rows, :].T - total[:, rows]
        if below is not None:
            source = source - dot(below, low[t])
        below = dot(source, inv[t])
        leaf[rows, :] = below.T


def gather_far(msg, far, relayed):
    out = [msg]
    for k in range(1, far):
        low = k & -k if relayed else k
        out.append(pair_swap(out[k - low], "row", 2 * low))
    return out


def gather_row(msg, far):
    out = []
    for piece in gather_far(msg, far, True):
        out += [piece, pair_swap(piece, "row", 1)]
    return out


def gather_stacked(msg, far):
    straight = gather_far(msg, far, False)
    mine, = call(stack_body, [shape(far, *msg.shape)], (), straight, stay=True)
    return (mine, pair_swap(mine, "row", 1)), range(far)


def per_device(rhs_leaf, rhs_anc, leaf_inv, leaf_low, couple, tile_cols, anc_inv, anc_low):
    leaf_tiles, tile, _ = leaf_inv.shape
    cols = rhs_leaf.shape[1]
    half = cols // 2
    count = lax.axis_size("row")
    far = count // 2
    decks = lax.axis_size("layer") // 2
    base = leaf_tiles * tile
    share = tile // lax.axis_size("layer")

    msg, right = call(
        leaf_body, (shape(base + 2 * share, cols), shape(half, tile)),
        (rhs_leaf, leaf_inv, leaf_low, anc_inv, anc_low, rhs_anc),
        scratch=[pltpu.VMEM((cols, tile), F32)], stay=True,
    )
    msgs = gather_row(msg, far)
    mats = merge(couple, tile_cols, leaf_tiles)
    columns = [mats[0]] + [pair_swap(mats[i], "row", i) for i in range(1, count)]

    own, other, mine = call(
        functools.partial(partial_body, count),
        [shape(half, tile)] * 2 + [shape(count, 2 * share, tile)],
        (), (*mats, *msgs), [pltpu.VMEM((cols, tile), F32)], stay=True,
    )
    part = own + pair_swap(other, "layer", 1)
    total = part
    for k in range(1, decks):
        total = total + pair_swap(part, "layer", 2 * k)
    pieces, piece_steps = gather_stacked(right - total, far)

    parts = []
    for k in range(decks):
        part = pair_swap(mine, "layer", 2 * k) if k else mine
        parts += [part, pair_swap(part, "layer", 1)]
    factors = call(
        factor_body,
        [shape(count, tile, 2 * tile, dtype=jnp.bfloat16)] * 4, (), parts,
        [pltpu.VMEM((count, tile, tile), F32)] * 2, stay=True,
    )
    z_mine, = call(
        functools.partial(solve_body, piece_steps), [shape(count, half, tile)],
        (), (*factors, *pieces), [pltpu.VMEM((count, half, tile), F32)], stay=True,
    )
    z_theirs = pair_swap(z_mine, "layer", 1)
    leaf, anc_out = call(
        functools.partial(final_body, count),
        (shape(base, cols), shape(tile, cols)),
        (leaf_inv, leaf_low), (z_mine, z_theirs, msg, *columns),
        [pltpu.VMEM((count, cols, tile), F32)],
    )
    return leaf, anc_out


def solution(mesh):
    placed = (
        P(("layer", "row"), None),
        P("row", None),
        P(("layer", "row"), None, None),
        P(("layer", "row"), None, None),
        P(("layer", "row"), None, None),
        P(("layer", "row"), None),
        P("row", None, None),
        P("row", None, None),
    )

    return jax.shard_map(
        per_device,
        mesh=mesh,
        in_specs=placed,
        out_specs=(P(("layer", "row"), None), P("row", None)),
        check_vma=False,
    )
```

```python
import functools
import math

import jax
import jax.numpy as jnp
from jax import lax
from jax.experimental import pallas as pl
from jax.experimental.pallas import tpu as pltpu
from jax.sharding import PartitionSpec as P


F32 = jnp.float32
VM = pl.BlockSpec(memory_space=pltpu.VMEM)
HB = pl.BlockSpec(memory_space=pltpu.HBM)
SM = pl.BlockSpec(memory_space=pltpu.SMEM)


def split(value, axis):
    high = value.astype(jnp.bfloat16)
    low = (value - high.astype(F32)).astype(jnp.bfloat16)
    return jnp.concatenate([high, low], axis=axis)


def spread(left, wide):
    rows, width = left.shape[0], wide.shape[1] // 2
    out = jnp.dot(split(left, 0), wide, preferred_element_type=F32)
    cross = out[:rows, width:] + out[rows:, :width]
    return out[:rows, :width] + (cross + out[rows:, width:])


def dot(left, right):
    return spread(left, split(right, 1))


def shape(*dims, dtype=F32):
    return jax.ShapeDtypeStruct(dims, dtype)


def room(scratch, outs=()):
    arrays = [v for v in [*scratch, *outs] if v.dtype in (F32, jnp.bfloat16)]
    size = sum(math.prod(v.shape) * jnp.dtype(v.dtype).itemsize for v in arrays)
    return pltpu.CompilerParams(vmem_limit_bytes=2 * size + (6 << 20))


def call(body, outs, far=(), arrived=(), scratch=(), stay=False, out_spec=VM):
    far = [pltpu.with_memory_space_constraint(v, pltpu.HBM) for v in far]
    arrived = [pltpu.with_memory_space_constraint(v, pltpu.VMEM) for v in arrived]
    if stay:
        outs = [pltpu.VMEM(o.shape, o.dtype) for o in outs]
    copies = [pltpu.VMEM(v.shape, v.dtype) for v in far]
    if far:
        copies.append(pltpu.SemaphoreType.DMA((len(far),)))
    scratch = copies + list(scratch)
    return pl.pallas_call(
        body, out_shape=list(outs), compiler_params=room(scratch, outs),
        in_specs=[HB] * len(far) + [VM] * len(arrived),
        out_specs=[out_spec] * len(outs), scratch_shapes=scratch,
    )(*far, *arrived)


def fetch(sources, copies):
    started = [
        pltpu.make_async_copy(source, target, copies[len(sources)].at[i])
        for i, (source, target) in enumerate(zip(sources, copies))
    ]
    for copy in started:
        copy.start()

    def ready(i):
        started[i].wait()
        return copies[i]

    return ready


def pair_swap(value, axis, distance):
    count = lax.axis_size(axis)
    return lax.ppermute(value, axis, [(i, i ^ distance) for i in range(count)])


def leaf_body(*refs):
    ready = fetch(refs[:6], refs[8:])
    inv_far, (msg, right) = refs[1], refs[6:8]
    buf = refs[-1]
    tile = msg.shape[1]
    tiles = inv_far.shape[0]
    half = tile // 2
    share = tile // lax.axis_size("layer")
    base = tiles * tile
    own = pl.multiple_of(lax.axis_index("layer") * share, share)
    start = pl.multiple_of(lax.axis_index("layer") % 2 * half, half)
    rhs, inv, low = ready(0), ready(1), ready(2)
    above = None
    for t in range(tiles):
        source = rhs[t * tile:(t + 1) * tile, :]
        if t > 0:
            source = source - dot(low[t - 1], above)
        above = dot(inv[t], source)
        msg[t * tile:(t + 1) * tile, :] = above
    msg[base:base + share, :] = ready(3)[0, pl.ds(own, share), :]
    msg[base + share:, :] = ready(4)[0, pl.ds(own, share), :]
    buf[...] = ready(5)[...].T
    right[...] = buf[pl.ds(start, half), :]


def merge_body(leaf_tiles, chunk, cols_far, couple, *rest):
    place = lax.axis_index("row")
    outs, (buf, acc_a, acc_b, cols, sems) = rest[:-5], rest[-5:]
    parts = couple.shape[0] // chunk
    table = pltpu.make_async_copy(cols_far, cols, sems.at[parts])
    table.start()
    started = [
        pltpu.make_async_copy(
            couple.at[pl.ds(i * chunk, chunk)], buf.at[pl.ds(i * chunk, chunk)], sems.at[i])
        for i in range(parts)
    ]
    for copy in started:
        copy.start()
    acc_a[...] = jnp.zeros_like(acc_a)
    acc_b[...] = jnp.zeros_like(acc_b)
    table.wait()

    def add(acc, k):
        col = cols[0, k]
        owner = lax.div(col, leaf_tiles)
        acc[(owner ^ place) * leaf_tiles + col - owner * leaf_tiles] += buf[k]

    for i in range(parts):
        started[i].wait()

        def one(j, carry):
            add(acc_a, i * chunk + 2 * j)
            add(acc_b, i * chunk + 2 * j + 1)
            return carry

        lax.fori_loop(0, chunk // 2, one, 0, unroll=4)
    for i, out in enumerate(outs):
        for t in range(leaf_tiles):
            out[t] = acc_a[i * leaf_tiles + t] + acc_b[i * leaf_tiles + t]


def merge(couple, cols, leaf_tiles):
    k_all, tile, _ = couple.shape
    rows = lax.axis_size("row")
    chunk = 16 if k_all % 16 == 0 else k_all
    acc = pltpu.VMEM((rows * leaf_tiles, tile, tile), F32)
    scratch = [pltpu.VMEM(couple.shape, F32), acc, acc]
    return pl.pallas_call(
        functools.partial(merge_body, leaf_tiles, chunk), name="merge",
        in_specs=[HB, HB],
        out_specs=[VM] * rows, out_shape=[pltpu.VMEM((leaf_tiles, tile, tile), F32)] * rows,
        compiler_params=room(scratch),
        scratch_shapes=scratch + [
            pltpu.SMEM(cols.shape, jnp.int32), pltpu.SemaphoreType.DMA((k_all // chunk + 1,))],
    )(*[pltpu.with_memory_space_constraint(v, pltpu.HBM) for v in (cols, couple)])


def partial_body(count, *refs):
    mats, msgs = refs[:count], refs[count:2 * count]
    own, other, mine, buf = refs[2 * count:]
    leaf_tiles, tile, _ = mats[0].shape
    half = tile // 2
    core = lax.axis_index("layer") % 2
    rights, highs, lows = [], [], []
    for i in range(count):
        mine[i] = msgs[i][leaf_tiles * tile:, :]
        rights.append(split(msgs[i][:leaf_tiles * tile, :], 1))
        row = jnp.concatenate([mats[i][t] for t in range(leaf_tiles)], axis=1)
        highs.append(row.astype(jnp.bfloat16))
        lows.append((row - highs[-1].astype(F32)).astype(jnp.bfloat16))
    right_side = jnp.concatenate(rights, axis=0)
    wide = jnp.dot(jnp.concatenate(highs, axis=1), right_side, preferred_element_type=F32)
    thin = jnp.dot(
        jnp.concatenate(lows, axis=1), right_side[:, :right_side.shape[1] // 2],
        preferred_element_type=F32,
    )
    cols = thin.shape[1]
    total = wide[:, :cols] + (wide[:, cols:] + thin)
    up = pl.multiple_of(core * half, half)
    down = pl.multiple_of((1 - core) * half, half)
    buf[...] = total.T
    own[...] = buf[pl.ds(up, half), :]
    other[...] = buf[pl.ds(down, half), :]


def stack_body(*refs):
    at = 0
    for ref in refs[:-1]:
        if len(ref.shape) == len(refs[-1].shape):
            refs[-1][at:at + ref.shape[0]] = ref[...]
            at += ref.shape[0]
        else:
            refs[-1][at] = ref[...]
            at += 1


def factor_body(*refs):
    parts = refs[:-8]
    at, a, tt, s, tt2, s2, a_buf, l_buf = refs[-8:]
    count, tile, _ = a_buf.shape
    share = tile // len(parts)
    layer = lax.axis_index("layer")
    place = lax.axis_index("row")
    for j, part in enumerate(parts):
        rows = pl.ds(pl.multiple_of((layer ^ j) * share, share), share)
        for i in range(count):
            a_buf[place ^ i, rows, :] = part[i, :share, :]
            l_buf[place ^ i, rows, :] = part[i, share:, :]
    for r in range(count):
        wide = split(a_buf[r], 1)
        a[r] = wide
        at[r] = split(a_buf[r].T, 1)
    ahead = [dot(a_buf[r], l_buf[r]).T if r else None for r in range(count)]
    behind = [spread(l_buf[r + 1], a[r]) if r < count - 1 else None for r in range(count)]
    for r in range(1, count):
        tt[r] = split(ahead[r], 1)
        s[r - 1] = split(behind[r - 1], 1)
    for r in range(2, count):
        tt2[r] = split(spread(ahead[r - 1], tt[r]), 1)
        s2[r - 2] = split(spread(behind[r - 1], s[r - 2]), 1)


def solve_body(steps, *refs):
    ready = fetch(refs[:2], refs[13:])
    at, a, tt, s, tt2, s2 = refs[2:8]
    right = refs[8:10]
    z, inv, low = refs[10:13]
    buf = refs[-1]
    count = buf.shape[0]
    place = lax.axis_index("row")
    for near in range(2):
        for p, k in enumerate(steps):
            buf[place ^ (2 * k + near)] = right[near][p]
    c = [spread(buf[r], at[r]) for r in range(count)]
    y = c[:1] + [c[r] - spread(c[r - 1], tt[r]) for r in range(1, count)]
    for r in range(2, count):
        y[r] = y[r] + spread(y[r - 2], tt2[r])
    d = [spread(y[r], a[r]) for r in range(count)]
    w = [d[r] - spread(d[r + 1], s[r]) for r in range(count - 1)] + d[-1:]
    for r in range(count - 3, -1, -1):
        w[r] = w[r] + spread(w[r + 2], s2[r])
    for r in range(count):
        z[r] = w[r]
    inv[...] = ready(0)[...]
    low[...] = ready(1)[...]


def couple_back(z_tiles, mats):
    cols = z_tiles[0].shape[0]
    left = jnp.concatenate([split(z, 0) for z in z_tiles], axis=1)
    rows = [jnp.concatenate([m[t] for t in range(m.shape[0])], axis=1) for m in mats]
    high = [row.astype(jnp.bfloat16) for row in rows]
    rest = [(row - h.astype(F32)).astype(jnp.bfloat16) for row, h in zip(rows, high)]
    both = jnp.dot(left, jnp.concatenate(high, axis=0), preferred_element_type=F32)
    single = jnp.dot(left[:cols], jnp.concatenate(rest, axis=0), preferred_element_type=F32)
    return both[:cols] + (both[cols:] + single)


def early_body(early, late, *refs):
    z_mine, z_theirs = refs[:2]
    mats = refs[2:2 + len(early)]
    total, z_late, anc, zt = refs[2 + len(early):]
    half = zt.shape[1] // 2
    core = lax.axis_index("layer") % 2
    place = lax.axis_index("row")
    zt[:, pl.ds(pl.multiple_of(core * half, half), half), :] = z_mine[...]
    zt[:, pl.ds(pl.multiple_of((1 - core) * half, half), half), :] = z_theirs[...]
    anc[...] = zt[place].T
    for j, i in enumerate(late):
        z_late[j] = zt[place ^ i]
    total[...] = couple_back([zt[place ^ i] for i in early], mats)


def final_body(late, *refs):
    inv, low, early, z_late, x = refs[:5]
    mats = refs[5:5 + late]
    leaf, leaf_buf, sems = refs[5 + late:]
    leaf_tiles, tile, _ = inv.shape
    total = early[...] + couple_back([z_late[j] for j in range(late)], mats)
    below, written = None, []
    for t in range(leaf_tiles - 1, -1, -1):
        rows = slice(t * tile, (t + 1) * tile)
        source = x[rows, :].T - total[:, rows]
        if below is not None:
            source = source - dot(below, low[t])
        below = dot(source, inv[t])
        leaf_buf[rows, :] = below.T
        written.append(pltpu.make_async_copy(
            leaf_buf.at[pl.ds(t * tile, tile)], leaf.at[pl.ds(t * tile, tile)], sems.at[t]))
        written[-1].start()
    for copy in written:
        copy.wait()


def gather_far(msg, far, relayed):
    out = [msg]
    for k in range(1, far):
        low = k & -k if relayed else k
        out.append(pair_swap(out[k - low], "row", 2 * low))
    return out


def gather_row(msg, far):
    out = []
    for piece in gather_far(msg, far, True):
        out += [piece, pair_swap(piece, "row", 1)]
    return out


def gather_stacked(msg, far):
    straight = gather_far(msg, far, False)
    mine, = call(stack_body, [shape(far, *msg.shape)], (), straight, stay=True)
    return (mine, pair_swap(mine, "row", 1)), range(far)


def per_device(rhs_leaf, rhs_anc, leaf_inv, leaf_low, couple, tile_cols, anc_inv, anc_low):
    leaf_tiles, tile, _ = leaf_inv.shape
    cols = rhs_leaf.shape[1]
    half = cols // 2
    count = lax.axis_size("row")
    far = count // 2
    decks = lax.axis_size("layer") // 2
    base = leaf_tiles * tile
    share = tile // lax.axis_size("layer")

    msg, right = call(
        leaf_body, (shape(base + 2 * share, cols), shape(half, tile)),
        (rhs_leaf, leaf_inv, leaf_low, anc_inv, anc_low, rhs_anc),
        scratch=[pltpu.VMEM((cols, tile), F32)], stay=True,
    )
    msgs = gather_row(msg, far)
    mats = merge(couple, tile_cols, leaf_tiles)
    columns = [mats[0]] + [pair_swap(mats[i], "row", i) for i in range(1, count)]

    own, other, mine = call(
        functools.partial(partial_body, count),
        [shape(half, tile)] * 2 + [shape(count, 2 * share, tile)],
        (), (*mats, *msgs), [pltpu.VMEM((cols, tile), F32)], stay=True,
    )
    part = own + pair_swap(other, "layer", 1)
    total = part
    for k in range(1, decks):
        total = total + pair_swap(part, "layer", 2 * k)
    pieces, piece_steps = gather_stacked(right - total, far)

    parts = []
    for k in range(decks):
        part = pair_swap(mine, "layer", 2 * k) if k else mine
        parts += [part, pair_swap(part, "layer", 1)]
    factors = call(
        factor_body,
        [shape(count, tile, 2 * tile, dtype=jnp.bfloat16)] * 6, (), parts,
        [pltpu.VMEM((count, tile, tile), F32)] * 2, stay=True,
    )
    z_mine, inv, low = call(
        functools.partial(solve_body, piece_steps),
        [shape(count, half, tile), shape(*leaf_inv.shape), shape(*leaf_low.shape)],
        (leaf_inv, leaf_low), (*factors, *pieces), [pltpu.VMEM((count, half, tile), F32)],
        stay=True,
    )
    z_theirs = pair_swap(z_mine, "layer", 1)
    late = [2 * k + 1 for k in range(far) if k & (k - 1)] or [count - 1]
    early = [i for i in range(count) if i not in late]
    summed, z_late, anc_out = call(
        functools.partial(early_body, early, late),
        [pltpu.VMEM((cols, base), F32), pltpu.VMEM((len(late), cols, tile), F32),
         shape(tile, cols)],
        (), (z_mine, z_theirs, *[columns[i] for i in early]),
        [pltpu.VMEM((count, cols, tile), F32)],
    )
    leaf, = call(
        functools.partial(final_body, len(late)), [shape(base, cols)],
        (), (inv, low, summed, z_late, msg, *[columns[i] for i in late]),
        [pltpu.VMEM((base, cols), F32), pltpu.SemaphoreType.DMA((leaf_tiles,))],
        out_spec=HB,
    )
    return leaf, anc_out


def solution(mesh):
    placed = (
        P(("layer", "row"), None),
        P("row", None),
        P(("layer", "row"), None, None),
        P(("layer", "row"), None, None),
        P(("layer", "row"), None, None),
        P(("layer", "row"), None),
        P("row", None, None),
        P("row", None, None),
    )

    return jax.shard_map(
        per_device,
        mesh=mesh,
        in_specs=placed,
        out_specs=(P(("layer", "row"), None), P("row", None)),
        check_vma=False,
    )
```
